256 devices in a mesh: img: 32 (over z, y), cls: 8 (over x, core).
Axes of the slice: x: 4, y: 4, z: 8, core: 2. Of those that a mesh axis runs over, the one named last changes fastest.
Arguments:
- embeddings: bfloat16 [3072, 1024], P('img'), may hold values from -128 to 128
- class_text_embedding: bfloat16 [1024, 21888], P(None, 'cls'), may hold values from -1 to 1
- neighbours: int32 [3072, 10], P('img'), may hold values from 0 to 607, as said below
- weights: float32 [3072, 10], P('img'), may hold values from 0.2 to 1
- requests: int32 [32, 32, 16], P('img'), may hold values from -1 to 95, as said below
Outputs:
- labels: float32 [3072, 21888], P('img', 'cls')
The draws below stay inside these ranges and needn't reach their ends.
Inputs may be any that keep to these rules, and one draw needn't show every extreme that they name: requests[d, p, j] is a row index within device p's 96 rows, or -1 for an empty slot; the live slots of each (d, p) come first; requests[d, d] is empty; every d fills all 16 slots for one p. `neighbours`: a slot of 96 or more names a live request slot of the row's own device.
All inputs are finite; a program needn't handle non-finite values.
Results may differ from the reference program's by a relative error of at most 0.00085.
Values may be sent and summed in bfloat16 or wider, within the bound.
A program may use at most 64 MiB of HBM per device.

```python
import math
import jax
import jax.numpy as jnp
from jax import lax

D = 1024
CLASS_COLUMNS = 21888
LIVE = 21841
ROW_DEV = 96
K = 10
CAP = 16
PEERS = 32
IMAGE_ROWS = 3072


def draw_embeddings(key, part):
    key_offset, key_scale = jax.random.split(jax.random.fold_in(key, 5))
    scale_factor = jnp.exp(jax.random.uniform(key_scale, (IMAGE_ROWS, 1), jnp.float32, math.log(0.15), math.log(1.5)))
    values = jnp.clip(jax.random.normal(key_offset, (IMAGE_ROWS, D), jnp.float32) * 3.0, -18.0, 18.0) * scale_factor
    return values.astype(jnp.bfloat16)


def draw_class_text_embedding(key, part):
    key_offset = jax.random.fold_in(jax.random.fold_in(key, 9), 0)
    values = jnp.clip(jax.random.normal(key_offset, (D, CLASS_COLUMNS), jnp.float32), -6.0, 6.0) / math.sqrt(D)
    return values.astype(jnp.bfloat16)


def graph_tables(key):
    keys = jax.random.split(jax.random.fold_in(key, 11), 9)
    counts = jax.random.randint(keys[0], (PEERS, PEERS), 0, CAP + 1)
    full_src = (jnp.arange(PEERS) + 1 + jax.random.randint(keys[1], (PEERS,), 0, PEERS - 1)) % PEERS
    chosen = jax.random.randint(keys[6], (), 0, PEERS - 1)
    full_src = jnp.where(jnp.arange(PEERS) == chosen, PEERS - 1, full_src)
    src_ids = jnp.arange(PEERS)
    counts = jnp.where(src_ids[None, :] == full_src[:, None], CAP, counts)
    counts = jnp.where(src_ids[None, :] == src_ids[:, None], 0, counts)
    slot = jnp.arange(CAP)
    asked = jax.random.randint(keys[2], (PEERS, PEERS, CAP), 0, ROW_DEV)
    requests = jnp.where(slot[None, None, :] < counts[:, :, None], asked, -1).astype(jnp.int32)
    livecount = jnp.sum(counts, axis=1)
    ending = jnp.cumsum(counts, axis=1)
    starting = ending - counts
    device = jnp.arange(IMAGE_ROWS) // ROW_DEV
    pick = jax.random.randint(keys[3], (IMAGE_ROWS, K), 0, 1 << 20) % livecount[device][:, None]
    source = jnp.sum(ending[device][:, None, :] <= pick[:, :, None], axis=-1)
    begin = jnp.take_along_axis(starting[device], source, axis=1)
    remote_slot = ROW_DEV + source * CAP + (pick - begin)
    local_slot = jax.random.randint(keys[4], (IMAGE_ROWS, K), 0, ROW_DEV)
    is_local = jax.random.randint(keys[5], (IMAGE_ROWS, K), 0, 2) == 0
    neighbours = jnp.where(is_local, local_slot, remote_slot)
    forced_row = chosen * ROW_DEV + jax.random.randint(keys[7], (), 0, ROW_DEV)
    forced_col = jax.random.randint(keys[8], (), 0, K)
    row_hit = (jnp.arange(IMAGE_ROWS) == forced_row)[:, None]
    column_ids = jnp.arange(K)[None, :]
    neighbours = jnp.where(row_hit & (column_ids == forced_col), ROW_DEV + PEERS * CAP - 1, neighbours)
    neighbours = jnp.where(row_hit & (column_ids == (forced_col + 1) % K), 0, neighbours)
    return (neighbours.astype(jnp.int32), requests)


def draw_neighbours(key, part):
    return graph_tables(key)[0]


def draw_requests(key, part):
    return graph_tables(key)[1]


def levels(rng, dims, cuts, low, high):
    loudness = 1.0
    for position, shards_of in cuts:
        steps = jax.random.uniform(jax.random.fold_in(jax.random.fold_in(rng, 6), position), (shards_of,), jnp.float32, low / len(cuts), high / len(cuts))
        loudness = loudness * jnp.repeat(jnp.exp(steps), dims[position] // shards_of).reshape((-1,) + (1,) * (len(dims) - 1 - position))
    return loudness


def setup_inputs(seed: int = 0) -> dict:
    key_list = jax.random.split(jax.random.key(seed), 6)
    return {
        "embeddings": draw_embeddings(jax.random.fold_in(key_list[5], 71), 0),
        "class_text_embedding": draw_class_text_embedding(jax.random.fold_in(key_list[5], 71), 0),
        "neighbours": draw_neighbours(jax.random.fold_in(key_list[5], 71), 0),
        "weights": jnp.clip(jnp.exp(math.log(1.0) - 1.609438 * jax.random.uniform(key_list[3], (IMAGE_ROWS, K), jnp.float32) ** levels(key_list[3], (IMAGE_ROWS, K), ((0, 32),), -0.2, 0.2)), 0.2, 1.0),
        "requests": draw_requests(jax.random.fold_in(key_list[5], 71), 0),
    }


smoothing = 1.0


def probabilities(block, class_text_embedding):
    logits = jnp.dot(block, class_text_embedding, preferred_element_type=jnp.float32)
    live = (jnp.arange(CLASS_COLUMNS) < LIVE)[None, :]
    masked = jnp.where(live, logits, -1e30)
    top = jnp.max(masked, axis=1, keepdims=True)
    powers = jnp.where(live, jnp.exp(masked - top), 0.0)
    total = jnp.sum(powers, axis=1, keepdims=True)
    return powers / total


def reference(embeddings, class_text_embedding, neighbours, weights, requests):
    blocks = embeddings.reshape(PEERS, ROW_DEV, D)
    first = lax.map(lambda b: probabilities(b, class_text_embedding), blocks).reshape(IMAGE_ROWS, CLASS_COLUMNS)
    device = (jnp.arange(IMAGE_ROWS) // ROW_DEV).astype(jnp.int32)[:, None]
    offset = neighbours - ROW_DEV
    remote = offset >= 0
    clipped = jnp.maximum(offset, 0)
    source = (clipped // CAP).astype(jnp.int32)
    within = (clipped % CAP).astype(jnp.int32)
    asked = requests[device, source, within]
    glob = jnp.where(remote, source * ROW_DEV + asked, device * ROW_DEV + neighbours).astype(jnp.int32)

    def sweep(previous):
        def one(items):
            index, edge, own = items
            acc = jnp.zeros((ROW_DEV, CLASS_COLUMNS), jnp.float32)
            for k in range(K):
                acc = acc + edge[:, k:k + 1] * previous[index[:, k]]
            degree = jnp.sum(edge, axis=1, keepdims=True)
            return (own + smoothing * acc) / (1.0 + smoothing * degree)

        return lax.map(one, (glob.reshape(PEERS, ROW_DEV, K), weights.reshape(PEERS, ROW_DEV, K),
                             first.reshape(PEERS, ROW_DEV, CLASS_COLUMNS))).reshape(IMAGE_ROWS, CLASS_COLUMNS)

    second = sweep(first)
    return sweep(second)
```

```python
import functools
import jax
import jax.numpy as jnp
from jax import lax
from jax.experimental import pallas as pl
from jax.experimental.pallas import tpu as pltpu
from jax.sharding import PartitionSpec as P

LIVE = 21841
ROWS = 96
K = 10
CAP = 16
PEERS = 32
ALL = ROWS * PEERS
D = 1024
N = 2736
TN = 256
CHUNK = 512
CHUNKS = ALL // CHUNK
SLOTS = K * 12
F32 = jnp.float32
BF16 = jnp.bfloat16


def dot(a, b):
    return jnp.dot(a, b, preferred_element_type=F32)


def split(x):
    hi = x.astype(BF16)
    return hi, (x - hi.astype(F32)).astype(BF16)


def place(peer, row):
    return peer * ROWS + row


def build_matrix(me, table, peer_ref, row_ref, w_ref, got, list_a, list_b, list_v, dense, m_ref):
    pos = place(peer_ref[...], row_ref[...])
    got[...] = jnp.zeros_like(got)

    def gather(step, carry):
        base = pl.multiple_of(step * 256, 256)
        lanes = lax.broadcasted_iota(jnp.int32, (ROWS, 256), 1) + base
        hot = [jnp.where(lanes == pos[:, k : k + 1], 1.0, 0.0).astype(BF16) for k in range(K)]
        got[...] += dot(jnp.concatenate(hot, axis=0), table(base, 256))
        return carry

    lax.fori_loop(0, ALL // 256, gather, 0)
    lanes = lax.broadcasted_iota(jnp.int32, (ROWS, 128), 1)
    w = w_ref[...]
    scale = 1.0 / (1.0 + jnp.sum(w, axis=1, keepdims=True))
    peers = jnp.zeros((ROWS, 128), F32)
    rows = jnp.zeros((ROWS, 128), F32)
    values = jnp.zeros((ROWS, 128), F32)
    for k in range(K):
        g = got[k * ROWS : (k + 1) * ROWS, :]
        live = lanes < K + 1
        value = (pltpu.roll(g, 128 - 32, 1) + pltpu.roll(g, 128 - 48, 1)) * w[:, k : k + 1]
        take = [g, pltpu.roll(g, 128 - 16, 1), value]
        take = [jnp.where(live, t, 0.0) for t in take]
        if k:
            take = [pltpu.roll(t, 12 * k, 1) for t in take]
        peers, rows, values = peers + take[0], rows + take[1], values + take[2]
    own = lanes == SLOTS
    peers = jnp.where(own, me.astype(F32), peers).astype(jnp.int32)
    rows = jnp.where(own, lax.broadcasted_iota(jnp.int32, (ROWS, 128), 0), rows.astype(jnp.int32))
    where = place(peers, rows)
    list_a[...] = where >> 7
    list_b[...] = where & 127
    list_v[...] = jnp.where(own, 1.0, values) * scale

    def scatter(r, carry):
        a, b, v = list_a[pl.ds(r, 1), :], list_b[pl.ds(r, 1), :], list_v[pl.ds(r, 1), :]
        left = jnp.where(lax.broadcasted_iota(jnp.int32, (32, 128), 0) == a, v, 0.0)
        right = jnp.where(lax.broadcasted_iota(jnp.int32, (128, 128), 0) == b, 1.0, 0.0).astype(BF16)
        both = jnp.concatenate(split(left), axis=0)
        out = lax.dot_general(both, right, (((1,), (1,)), ((), ())), preferred_element_type=F32)
        dense[pl.ds(r, 24, stride=ROWS), :] = out[:24] + out[32:56]
        return carry

    lax.fori_loop(0, ROWS, scatter, 0, unroll=8)
    per = CHUNK // 128
    for i in range(CHUNKS):
        block = jnp.concatenate([dense[(per * i + j) * ROWS : (per * i + j + 1) * ROWS, :] for j in range(per)], axis=1)
        hi, lo = split(block)
        m_ref[i, :ROWS] = hi
        m_ref[i, ROWS:] = lo


def tiles():
    return [(off, min(TN, N - off)) for off in range(0, N, TN)]


def logits_tile(e_ref, c_ref, buf, chunk, slot, off, width):
    rows = pl.ds(pl.multiple_of(chunk * CHUNK, CHUNK), CHUNK)
    buf[slot, :, off : off + width] = dot(e_ref[rows, :D], c_ref[:, off : off + width])


def label_tile(lse_ref, m_ref, buf, acc, chunk, slot, off, width):
    rows = pl.ds(pl.multiple_of(chunk * CHUNK, CHUNK), CHUNK)
    lse = lse_ref[rows, :]
    lse = jnp.concatenate([lse] * (-(-width // 128)), axis=1)[:, :width]
    hi, lo = split(jnp.exp(buf[slot, :, off : off + width] - lse))
    m = m_ref[chunk]
    a = dot(m, hi)
    acc[:, off : off + width] += a[:ROWS] + a[ROWS:] + dot(m[:ROWS], lo)


def kernel(e_ref, c_ref, lse_ref, peer_ref, row_ref, w_ref, o_ref, buf, acc, got, list_a, list_b, list_v, dense, m_ref):
    me = lax.axis_index("img")
    build_matrix(me, lambda base, n: e_ref[pl.ds(base, n), D:], peer_ref, row_ref, w_ref, got, list_a, list_b, list_v, dense, m_ref)
    acc[...] = jnp.zeros_like(acc)
    for off, width in tiles():
        logits_tile(e_ref, c_ref, buf, 0, 0, off, width)

    def step(i, carry):
        slot = lax.rem(i, 2)
        for off, width in tiles():
            logits_tile(e_ref, c_ref, buf, i + 1, 1 - slot, off, width)
            label_tile(lse_ref, m_ref, buf, acc, i, slot, off, width)
        return carry

    lax.fori_loop(0, CHUNKS - 1, step, 0)
    column = lax.axis_index("cls") * N
    for off, width in tiles():
        label_tile(lse_ref, m_ref, buf, acc, CHUNKS - 1, (CHUNKS - 1) % 2, off, width)
        here = column + off + lax.broadcasted_iota(jnp.int32, (ROWS, width), 1)
        o_ref[:, off : off + width] = jnp.where(here < LIVE, acc[:, off : off + width], 0.0)


def shards(embeddings, class_text_embedding, neighbours, weights, requests):
    me = lax.axis_index("img")
    live = (lax.axis_index("cls") * N + jnp.arange(N) < LIVE)[None, :]
    offset = neighbours - ROWS
    hot = jnp.maximum(offset, 0)[:, :, None] == jnp.arange(PEERS * CAP)
    asked = jnp.sum(jnp.where(hot, requests.reshape(PEERS * CAP), 0), axis=2)
    peer = jnp.where(offset >= 0, jnp.maximum(offset, 0) // CAP, me)
    row = jnp.where(offset >= 0, asked, neighbours)
    scale = 1.0 / (1.0 + jnp.sum(weights, axis=1, keepdims=True))
    value_hi, value_lo = split(jnp.concatenate([scale, weights * scale], axis=1))
    own_row = jnp.arange(ROWS, dtype=jnp.int32)[:, None]
    peers = jnp.concatenate([jnp.full((ROWS, 1), me, jnp.int32), peer], axis=1).astype(BF16)
    rows = jnp.concatenate([own_row, row], axis=1).astype(BF16)
    gap = jnp.zeros((ROWS, 16 - (K + 1)), BF16)
    table = jnp.concatenate([peers, gap, rows, gap, value_hi, gap, value_lo, gap, jnp.zeros((ROWS, 64), BF16)], axis=1)
    extended = lax.all_gather(jnp.concatenate([embeddings, table], axis=1), "img", axis=0, tiled=True)

    logits = jnp.where(live, dot(embeddings, class_text_embedding), -1e30)
    top = lax.pmax(jnp.max(logits, axis=1), "cls")
    total = lax.psum(jnp.sum(jnp.where(live, jnp.exp(logits - top[:, None]), 0.0), axis=1), "cls")
    lse = lax.all_gather(top + jnp.log(total), "img", axis=0, tiled=True)
    lse = jnp.broadcast_to(lse[:, None], (ALL, 128))

    vmem = pl.BlockSpec(memory_space=pltpu.VMEM)
    return pl.pallas_call(
        kernel,
        out_shape=jax.ShapeDtypeStruct((ROWS, N), F32),
        in_specs=[vmem] * 6,
        out_specs=vmem,
        scratch_shapes=[
            pltpu.VMEM((2, CHUNK, N), F32),
            pltpu.VMEM((ROWS, N), F32),
            pltpu.VMEM((K * ROWS, 128), F32),
            pltpu.VMEM((ROWS, 128), jnp.int32),
            pltpu.VMEM((ROWS, 128), jnp.int32),
            pltpu.VMEM((ROWS, 128), F32),
            pltpu.VMEM((24 * ROWS, 128), F32),
            pltpu.VMEM((CHUNKS, 2 * ROWS, CHUNK), BF16),
        ],
        compiler_params=pltpu.CompilerParams(vmem_limit_bytes=56 << 20),
    )(extended, class_text_embedding, lse, peer, row, weights)


def solution(mesh):
    in_specs = (
        P("img", None),
        P(None, "cls"),
        P("img", None),
        P("img", None),
        P("img", None, None),
    )
    return jax.shard_map(shards, mesh=mesh, in_specs=in_specs, out_specs=P("img", "cls"), check_vma=False)
```

```python
import jax
import jax.numpy as jnp
from jax import lax
from jax.experimental import pallas as pl
from jax.experimental.pallas import tpu as pltpu
from jax.sharding import PartitionSpec as P

LIVE = 21841
ROWS = 96
HALF = 48
K = 10
PEERS = 32
CLS = 8
ALL = ROWS * PEERS
D = 1024
N = 2736
TN = 256
CHUNK = 512
CHUNKS = ALL // CHUNK
PACK = 32
F32 = jnp.float32
BF16 = jnp.bfloat16
MESH = pl.DeviceIdType.MESH
TILES = [(off, min(TN, N - off)) for off in range(0, N, TN)]
B_BASE = (0, 1536, 2048, 2560)
A_BASE = 512
MESSAGES = 40


def dot(a, b):
    return jnp.dot(a, b, preferred_element_type=F32)


def dot_nt(a, b):
    return lax.dot_general(a, b, (((1,), (1,)), ((), ())), preferred_element_type=F32)


def split(x):
    hi = x.astype(BF16)
    return hi, (x - hi.astype(F32)).astype(BF16)


def iota(shape, axis):
    return lax.broadcasted_iota(jnp.int32, shape, axis)


def relative(z, y, peer):
    return ((peer >> 2) - z) & 7, ((peer & 3) - y) & 3


def place(z, y, peer, row):
    dz, dy = relative(z, y, peer)
    zi = jnp.where(dz == 0, 0, jnp.where(dz <= 4, 2 * dz - 1, 16 - 2 * dz))
    yi = jnp.where(dy < 2, dy, 5 - dy)
    half = jnp.where(row >= HALF, 1, 0)
    t = row - HALF * half
    in_a = A_BASE + half * 512 + zi * 64 + yi * 16 + t
    in_b = jnp.where(yi == 0, 0, 1024 + 512 * yi) + half * 256 + zi * 32 + t - 16
    return jnp.where(t < 16, in_a, in_b)


def kernel(
    e_ref, ct_hbm, near_ref, w_ref, ask_ref, o_ref,
    every, ct, buf0, buf1, acc, lse_ref, m_ref, dense, table, all_tables, own, xs, ys, lists_a, lists_b, lists_v, got, stats, lses,
    ct_sem, ssem, rsem, table_sem, stat_sem, lse_sem, m_sem,
):
    me, c = lax.axis_index("img"), lax.axis_index("cls")
    z, y, h = me // 4, lax.rem(me, 4), lax.rem(c, 2)
    bufs = (buf0, buf1)

    load_ct = pltpu.make_async_copy(ct_hbm, ct, ct_sem)
    load_ct.start()

    barrier = pltpu.get_barrier_semaphore()

    def greet_img(j, carry):
        pl.semaphore_signal(barrier, inc=1, device_id={"img": lax.rem(me + j, PEERS)}, device_id_type=MESH)
        return carry

    def greet_cls(j, carry):
        pl.semaphore_signal(barrier, inc=1, device_id={"cls": lax.rem(c + j, CLS)}, device_id_type=MESH)
        return carry

    lax.fori_loop(1, PEERS, greet_img, 0)
    lax.fori_loop(1, CLS, greet_cls, 0)

    for half in range(2):
        every[A_BASE + 512 * half : A_BASE + 512 * half + 16, :] = e_ref[HALF * half : HALF * half + 16, :]
        every[256 * half : 256 * half + 32, :] = e_ref[HALF * half + 16 : HALF * half + HALF, :]

    near = near_ref[...]
    w_t = w_ref[...]
    far = jnp.maximum(near - ROWS, 0)
    source, within = far >> 4, far & 15
    asks = ask_ref[...].astype(F32).astype(BF16)
    ys[...] = jnp.zeros_like(ys)
    ys[0:K, 0:ROWS] = jnp.where(near >= ROWS, source, me).astype(F32)
    for k in range(K):
        hot = jnp.where(iota((PEERS, ROWS), 0) == source[k : k + 1, :], 1.0, 0.0).astype(BF16)
        picked = dot(asks, hot)
        asked = jnp.sum(jnp.where(iota((16, ROWS), 0) == within[k : k + 1, :], picked, 0.0), axis=0, keepdims=True)
        ys[16 + k : 17 + k, 0:ROWS] = jnp.where(near[k : k + 1, :] >= ROWS, asked, near[k : k + 1, :].astype(F32))
    ys[32 : 32 + K, 0:ROWS] = w_t
    w_hi = w_t.astype(BF16).astype(F32)
    pieces = [ys[0:K, 0:ROWS], ys[16 : 16 + K, 0:ROWS], w_hi, w_t - w_hi]
    xs[...] = jnp.zeros_like(xs)
    for q in range(3):
        for i, piece in enumerate(pieces):
            at = q * 4 * K + i * K
            xs[at : at + K, 0:PACK] = piece[:, q * PACK : (q + 1) * PACK]
    table[...] = xs[...].T[:PACK, :].astype(BF16)
    all_tables[0:PACK, :] = table[...]
    own[...] = ys[...].T

    pl.semaphore_wait(barrier, PEERS - 1 + CLS - 1)

    def peer_at(j):
        return {"img": lax.rem(z + 8 - j // 4, 8) * 4 + lax.rem(y + 4 - lax.rem(j, 4), 4)}

    def table_copy(j, n):
        rows = pl.ds(pl.multiple_of(j * PACK, PACK), n * PACK)
        src = table if n == 1 else all_tables.at[rows]
        return pltpu.make_async_remote_copy(src, all_tables.at[rows], table_sem.at[0], table_sem.at[1], device_id=peer_at(j), device_id_type=MESH)

    def send_table(j, carry):
        table_copy(j, 1).start()
        return carry

    lax.fori_loop(1, PEERS, send_table, 0)

    y_up, y_down = {"img": z * 4 + lax.rem(y + 1, 4)}, {"img": z * 4 + lax.rem(y + 3, 4)}
    z_up, z_down = {"img": lax.rem(z + 1, 8) * 4 + y}, {"img": lax.rem(z + 7, 8) * 4 + y}
    sibling = {"cls": c + 1 - 2 * h}
    made = {}

    def go(name, src, dst, n, target, columns=slice(None)):
        i = len(made)
        src = pl.ds(pl.multiple_of(src, 16), n)
        dst = pl.ds(pl.multiple_of(dst, 16), n)
        copy = pltpu.make_async_remote_copy(
            every.at[src, columns], every.at[dst, columns], ssem.at[i], rsem.at[i], device_id=target, device_id_type=MESH
        )
        copy.start()
        made[name] = copy

    def take(*names):
        for name in names:
            made[name].wait_recv()

    def at_a(zi, yi=0):
        return A_BASE + 512 * h + 64 * zi + 16 * yi

    def at_b(yi, zi=0):
        return B_BASE[yi] + 256 * h + 32 * zi

    def share(name, at, n):
        go(name, at, at, n, sibling)

    def round_0():
        go("a_y2", at_a(0), at_a(0, 2), 16, y_up)
        go("a_y1", at_a(0), at_a(0, 1), 16, y_down)
        go("b_z2", at_b(0), at_b(0, 2), 32, z_up)
        go("b_z1", at_b(0), at_b(0, 1), 32, z_down)

    def round_1():
        take("a_y1", "a_y2", "b_z1", "b_z2")
        go("a_y3u", at_a(0, 2), at_a(0, 3), 16, y_up, slice(0, 512))
        go("a_y3d", at_a(0, 1), at_a(0, 3), 16, y_down, slice(512, 1024))
        go("b_z4", at_b(0, 2), at_b(0, 4), 32, z_up)
        go("b_z3", at_b(0, 1), at_b(0, 3), 32, z_down)
        go("b_y2q0", at_b(0), at_b(2), 96, y_up)
        go("b_y1q0", at_b(0), at_b(1), 96, y_down)

    def round_2():
        take("a_y3u", "a_y3d", "b_z3", "b_z4")
        go("a_z2", at_a(0), at_a(2), 64, z_up)
        go("a_z1", at_a(0), at_a(1), 64, z_down)
        go("b_z6", at_b(0, 4), at_b(0, 6), 32, z_up)
        go("b_z5", at_b(0, 3), at_b(0, 5), 32, z_down)
        share("a_s0", at_a(0, 1), 48)

    def round_3():
        take("b_z5", "b_z6")
        go("b_z7u", at_b(0, 6), at_b(0, 7), 16, z_up)
        go("b_z7d", at_b(0, 5) + 16, at_b(0, 7) + 16, 16, z_down)
        take("a_z1", "a_z2")
        go("a_z4", at_a(2), at_a(4), 64, z_up)
        go("a_z3", at_a(1), at_a(3), 64, z_down)
        share("a_s1", at_a(1), 128)

    def round_4():
        take("b_z7u", "b_z7d")
        go("b_y2q1", at_b(0, 3), at_b(2, 3), 160, y_up)
        go("b_y1q1", at_b(0, 3), at_b(1, 3), 160, y_down)
        share("b_s0", at_b(0, 1), 224)
        take("a_z3", "a_z4")
        go("a_z6", at_a(4), at_a(6), 64, z_up)
        go("a_z5", at_a(3), at_a(5), 64, z_down)
        share("a_s3", at_a(3), 128)

    def round_5():
        take("b_y1q0", "b_y2q0")
        go("b_y3q0u", at_b(2), at_b(3), 48, y_up)
        go("b_y3q0d", at_b(1) + 48, at_b(3) + 48, 48, y_down)
        take("a_z5", "a_z6")
        go("a_z7u", at_a(6), at_a(7), 32, z_up)
        go("a_z7d", at_a(5) + 32, at_a(7) + 32, 32, z_down)

    def round_6():
        take("a_z7u", "a_z7d")
        share("a_s5", at_a(5), 192)

    def round_7():
        take("b_y1q1", "b_y2q1")
        go("b_y3q1u", at_b(2, 3), at_b(3, 3), 80, y_up)
        go("b_y3q1d", at_b(1, 3) + 80, at_b(3, 3) + 80, 80, y_down)
        share("b_s1", at_b(1), 256)
        share("b_s2", at_b(2), 256)

    def round_8():
        take("b_y3q0u", "b_y3q0d", "b_y3q1u", "b_y3q1d")
        share("b_s3", at_b(3), 256)

    round_0()

    load_ct.wait()
    column = c * N
    top = jnp.full((ROWS, 1), -1e30, F32)
    for off, width in TILES:
        logits = dot_nt(e_ref[...], ct[off : off + width, :])
        logits = jnp.where(column + off + iota((ROWS, width), 1) < LIVE, logits, -1e30)
        buf1[0:ROWS, off : off + width] = logits
        top = jnp.maximum(top, jnp.max(logits, axis=1, keepdims=True))
    round_1()
    total = jnp.zeros((ROWS, 1), F32)
    for off, width in TILES:
        total += jnp.sum(jnp.exp(buf1[0:ROWS, off : off + width] - top), axis=1, keepdims=True)
    lanes = iota((ROWS, 128), 1)
    xs[...] = jnp.zeros_like(xs)
    xs[0:ROWS, :] = jnp.where(lanes == 0, top, jnp.where(lanes == 1, total, 0.0))
    stats[0] = xs[...].T[:8, :]

    def stat_copy(j, n):
        src = stats.at[0] if n == 1 else stats.at[pl.ds(j, n)]
        dst = stats.at[j] if n == 1 else stats.at[pl.ds(j, n)]
        return pltpu.make_async_remote_copy(
            src, dst, stat_sem.at[0], stat_sem.at[1], device_id={"cls": lax.rem(c + j, CLS)}, device_id_type=MESH
        )

    def send_stat(j, carry):
        stat_copy(j, 1).start()
        return carry

    lax.fori_loop(1, CLS, send_stat, 0)
    round_2()

    table_copy(1, PEERS - 1).wait_recv()
    mine = own[pl.ds(pl.multiple_of(HALF * h, 16), HALF), :]
    lanes = iota((HALF, 128), 1)
    peer = mine.astype(jnp.int32)
    row = pltpu.roll(mine, 128 - 16, 1).astype(jnp.int32)
    weight = pltpu.roll(mine, 128 - 32, 1)
    scale = 1.0 / (1.0 + jnp.sum(jnp.where(lanes < K, weight, 0.0), axis=1, keepdims=True))
    dz, dy = relative(z, y, peer)
    packed = (dz * 4 + dy) * PACK + (row & (PACK - 1))
    group = row >> 5
    for step in range(4):
        at = iota((HALF, 256), 1) + step * 256
        hot = [jnp.where(at == packed[:, k : k + 1], 1.0, 0.0).astype(BF16) for k in range(K)]
        part = dot(jnp.concatenate(hot, axis=0), all_tables[step * 256 : step * 256 + 256, :])
        got[...] = part if step == 0 else got[...] + part
    peers = jnp.zeros((HALF, 128), F32)
    rows = jnp.zeros((HALF, 128), F32)
    values = jnp.zeros((HALF, 128), F32)
    for k in range(K):
        g = got[k * HALF : (k + 1) * HALF, :]
        q = group[:, k : k + 1]
        g = jnp.where(q == 0, g, jnp.where(q == 1, pltpu.roll(g, 128 - 4 * K, 1), pltpu.roll(g, 128 - 8 * K, 1)))
        edge = jnp.where(lanes < K, pltpu.roll(g, 128 - 2 * K, 1) + pltpu.roll(g, 128 - 3 * K, 1), 0.0)
        outer = weight[:, k : k + 1] / (1.0 + jnp.sum(edge, axis=1, keepdims=True))
        self_lane = lanes == K
        pk = jnp.where(self_lane, peer[:, k : k + 1].astype(F32), jnp.where(lanes < K, g, 0.0))
        rk = jnp.where(self_lane, row[:, k : k + 1].astype(F32), jnp.where(lanes < K, pltpu.roll(g, 128 - K, 1), 0.0))
        vk = jnp.where(self_lane, outer, edge * outer)
        if k:
            pk, rk, vk = pltpu.roll(pk, 12 * k, 1), pltpu.roll(rk, 12 * k, 1), pltpu.roll(vk, 12 * k, 1)
        peers, rows, values = peers + pk, rows + rk, values + vk
    itself = lanes == 12 * K
    peers = jnp.where(itself, me, peers.astype(jnp.int32))
    rows = jnp.where(itself, HALF * h + iota((HALF, 128), 0), rows.astype(jnp.int32))
    where = place(z, y, peers, rows)
    lists_a[...] = where >> 7
    lists_b[...] = where & 127
    lists_v[...] = jnp.where(itself, 1.0, values) * scale
    round_3()

    stat_copy(1, CLS - 1).wait_recv()
    top = stats[0, 0:1, :]
    for j in range(1, CLS):
        top = jnp.maximum(top, stats[j, 0:1, :])
    total = jnp.zeros((1, 128), F32)
    for j in range(CLS):
        total += stats[j, 1:2, :] * jnp.exp(stats[j, 0:1, :] - top)
    lses[0] = top + jnp.log(total)

    def lse_copy(j, n):
        src = lses.at[0] if n == 1 else lses.at[pl.ds(j, n)]
        dst = lses.at[j] if n == 1 else lses.at[pl.ds(j, n)]
        return pltpu.make_async_remote_copy(src, dst, lse_sem.at[0], lse_sem.at[1], device_id=peer_at(j), device_id_type=MESH)

    def send_lse(j, carry):
        lse_copy(j, 1).start()
        return carry

    lax.fori_loop(1, PEERS, send_lse, 0)

    def scatter(r, carry):
        a, b, v = lists_a[pl.ds(r, 1), :], lists_b[pl.ds(r, 1), :], lists_v[pl.ds(r, 1), :]
        left = jnp.where(iota((32, 128), 0) == a, v, 0.0)
        right = jnp.where(iota((128, 128), 0) == b, 1.0, 0.0).astype(BF16)
        out = dot_nt(jnp.concatenate(split(left), axis=0), right)
        dense[pl.ds(r, 24, stride=HALF), :] = out[:24] + out[32:56]
        return carry

    lax.fori_loop(0, HALF, scatter, 0, unroll=8)
    per = CHUNK // 128
    mine_hi = pl.ds(pl.multiple_of(HALF * h, 16), HALF)
    mine_lo = pl.ds(pl.multiple_of(HALF * h + ROWS, 16), HALF)
    for i in range(CHUNKS):
        block = jnp.concatenate([dense[(per * i + j) * HALF : (per * i + j + 1) * HALF, :] for j in range(per)], axis=1)
        hi, lo = split(block)
        m_ref[i, mine_hi, :] = hi
        m_ref[i, mine_lo, :] = lo
    m_copies = [
        pltpu.make_async_remote_copy(
            m_ref.at[:, part, :], m_ref.at[:, part, :], m_sem.at[i, 0], m_sem.at[i, 1], device_id=sibling, device_id_type=MESH
        )
        for i, part in enumerate((mine_hi, mine_lo))
    ]
    for copy in m_copies:
        copy.start()
    round_4()

    lse_copy(1, PEERS - 1).wait_recv()
    xs[...] = jnp.zeros_like(xs)
    xs[0:PEERS, :] = lses[:, 0, :]
    ys[...] = xs[...].T
    for dz in range(8):
        for dy in range(4):
            zi = 0 if dz == 0 else 2 * dz - 1 if dz <= 4 else 16 - 2 * dz
            yi = dy if dy < 2 else 5 - dy
            for half in range(2):
                col = jnp.broadcast_to(ys[HALF * half : HALF * half + HALF, dz * 4 + dy : dz * 4 + dy + 1], (HALF, 128))
                a = A_BASE + 512 * half + 64 * zi + 16 * yi
                b = B_BASE[yi] + 256 * half + 32 * zi
                lse_ref[a : a + 16, :] = col[:16]
                lse_ref[b : b + 32, :] = col[16:]
    acc[...] = jnp.zeros_like(acc)
    round_5()
    take("b_s0")

    def logits_tile(chunk, off, width):
        bufs[chunk % 2][:, off : off + width] = dot_nt(every[chunk * CHUNK : (chunk + 1) * CHUNK, :], ct[off : off + width, :])

    def label_tile(chunk, off, width):
        lse = lse_ref[chunk * CHUNK : (chunk + 1) * CHUNK, :]
        lse = jnp.concatenate([lse] * (-(-width // 128)), axis=1)[:, :width]
        hi, lo = split(jnp.exp(bufs[chunk % 2][:, off : off + width] - lse))
        m = m_ref[chunk]
        a = dot(m, hi)
        acc[:, off : off + width] += a[:ROWS] + a[ROWS:] + dot(m[:ROWS], lo)

    for off, width in TILES:
        logits_tile(0, off, width)
    for copy in m_copies:
        copy.wait_recv()
    round_6()
    take("a_s0", "a_s1", "a_s3", "a_s5")
    before = {0: [], 1: [round_7], 2: [round_8, lambda: take("b_s1")], 3: [lambda: take("b_s2")], 4: [lambda: take("b_s3")]}
    for chunk in range(CHUNKS):
        for event in before.get(chunk, []):
            event()
        for off, width in TILES:
            if chunk + 1 < CHUNKS:
                logits_tile(chunk + 1, off, width)
            label_tile(chunk, off, width)
    for off, width in TILES:
        here = column + off + iota((ROWS, width), 1)
        o_ref[:, off : off + width] = jnp.where(here < LIVE, acc[:, off : off + width], 0.0)

    for copy in made.values():
        copy.wait_send()
    for copy in m_copies:
        copy.wait_send()
    table_copy(1, PEERS - 1).wait_send()
    stat_copy(1, CLS - 1).wait_send()
    lse_copy(1, PEERS - 1).wait_send()


def shards(embeddings, class_text_embedding, neighbours, weights, requests):
    vmem = pl.BlockSpec(memory_space=pltpu.VMEM)
    dma = pltpu.SemaphoreType.DMA
    return pl.pallas_call(
        kernel,
        out_shape=jax.ShapeDtypeStruct((ROWS, N), F32),
        in_specs=[vmem, pl.BlockSpec(memory_space=pl.ANY), vmem, vmem, vmem],
        out_specs=vmem,
        scratch_shapes=[
            pltpu.VMEM((ALL, D), BF16),
            pltpu.VMEM((N, D), BF16),
            pltpu.VMEM((CHUNK, N), F32),
            pltpu.VMEM((CHUNK, N), F32),
            pltpu.VMEM((ROWS, N), F32),
            pltpu.VMEM((ALL, 128), F32),
            pltpu.VMEM((CHUNKS, 2 * ROWS, CHUNK), BF16),
            pltpu.VMEM((24 * HALF, 128), F32),
            pltpu.VMEM((PACK, 128), BF16),
            pltpu.VMEM((PEERS * PACK, 128), BF16),
            pltpu.VMEM((128, 128), F32),
            pltpu.VMEM((128, 128), F32),
            pltpu.VMEM((128, 128), F32),
            pltpu.VMEM((HALF, 128), jnp.int32),
            pltpu.VMEM((HALF, 128), jnp.int32),
            pltpu.VMEM((HALF, 128), F32),
            pltpu.VMEM((K * HALF, 128), F32),
            pltpu.VMEM((CLS, 8, 128), F32),
            pltpu.VMEM((PEERS, 1, 128), F32),
            dma,
            dma((MESSAGES,)),
            dma((MESSAGES,)),
            dma((2,)),
            dma((2,)),
            dma((2,)),
            dma((2, 2)),
        ],
        compiler_params=pltpu.CompilerParams(vmem_limit_bytes=56 << 20, collective_id=0, has_side_effects=True),
    )(embeddings, class_text_embedding.T, neighbours.T, weights.T, requests[0].T)


def solution(mesh):
    in_specs = (
        P("img", None),
        P(None, "cls"),
        P("img", None),
        P("img", None),
        P("img", None, None),
    )
    return jax.shard_map(shards, mesh=mesh, in_specs=in_specs, out_specs=P("img", "cls"), check_vma=False)
```

```python
import jax
import jax.numpy as jnp
from jax import lax
from jax.experimental import pallas as pl
from jax.experimental.pallas import tpu as pltpu
from jax.sharding import PartitionSpec as P

LIVE = 21841
ROWS = 96
HALF = 48
K = 10
PEERS = 32
CLS = 8
ALL = ROWS * PEERS
D = 1024
N = 2736
TN = 256
PACK = 32
F32 = jnp.float32
BF16 = jnp.bfloat16
MESH = pl.DeviceIdType.MESH
TILES = [(off, min(TN, N - off)) for off in range(0, N, TN)]
A_AT = [(0, 1152)] + [(s + 64 * i, 128) for s in (512, 1280, 1792) for i in range(2)] + [(2304, 64)]
B_AT = [
    [(64 + 32 * i, 224) for i in range(7)] + [(1216, 32)],
    [(768 + 32 * i, 96) for i in range(3)] + [(s + 32 * i, 64) for s in (1536, 2048) for i in range(2)] + [(2432, 32)],
    [(960 + 32 * i, 96) for i in range(3)] + [(s + 32 * i, 64) for s in (1664, 2176) for i in range(2)] + [(2496, 32)],
    [(2816 + 32 * i, 96) for i in range(3)] + [(2560 + 32 * i, 128) for i in range(4)] + [(3008, 32)],
]
CHUNK_AT = (0, 512, 1152, 1792, 2304, 2816, 3072)
CHUNKS = 6
CHUNK = 640
MESSAGES = 72


def dot(a, b):
    return jnp.dot(a, b, preferred_element_type=F32)


def dot_nt(a, b):
    return lax.dot_general(a, b, (((1,), (1,)), ((), ())), preferred_element_type=F32)


def split(x):
    hi = x.astype(BF16)
    return hi, (x - hi.astype(F32)).astype(BF16)


def iota(shape, axis):
    return lax.broadcasted_iota(jnp.int32, shape, axis)


def relative(z, y, peer):
    return ((peer >> 2) - z) & 7, ((peer & 3) - y) & 3


def place(z, y, peer, row):
    dz, dy = relative(z, y, peer)
    zi = jnp.where(dz == 0, 0, jnp.where(dz <= 4, 2 * dz - 1, 16 - 2 * dz))
    yi = jnp.where(dy < 2, dy, 5 - dy)
    half = jnp.where(row >= HALF, 1, 0)
    t = row - HALF * half
    a, b = jnp.zeros_like(t), jnp.zeros_like(t)
    for i in range(8):
        a = jnp.where(zi == i, A_AT[i][0] + A_AT[i][1] * half, a)
        for j in range(4):
            b = jnp.where(jnp.logical_and(zi == i, yi == j), B_AT[j][i][0] + B_AT[j][i][1] * half, b)
    return jnp.where(t < 16, a + 16 * yi + t, b + t - 16)


def kernel(
    e_ref, ct_hbm, near_ref, w_ref, ask_ref, o_ref,
    every, ct, buf0, buf1, acc, lse_ref, m_ref, dense, table, all_tables, own, xs, ys, lists_a, lists_b, lists_v, got, stats, lses,
    ct_sem, ssem, rsem, table_sem, stat_sem, lse_sem, m_sem,
):
    me, c = lax.axis_index("img"), lax.axis_index("cls")
    z, y, h = me // 4, lax.rem(me, 4), lax.rem(c, 2)
    bufs = (buf0, buf1)

    load_ct = pltpu.make_async_copy(ct_hbm, ct, ct_sem)
    load_ct.start()

    barrier = pltpu.get_barrier_semaphore()

    def greet_img(j, carry):
        pl.semaphore_signal(barrier, inc=1, device_id={"img": lax.rem(me + j, PEERS)}, device_id_type=MESH)
        return carry

    def greet_cls(j, carry):
        pl.semaphore_signal(barrier, inc=1, device_id={"cls": lax.rem(c + j, CLS)}, device_id_type=MESH)
        return carry

    lax.fori_loop(1, PEERS, greet_img, 0)
    lax.fori_loop(1, CLS, greet_cls, 0)

    for half in range(2):
        a, b = A_AT[0][0] + A_AT[0][1] * half, B_AT[0][0][0] + B_AT[0][0][1] * half
        every[a : a + 16, :] = e_ref[HALF * half : HALF * half + 16, :]
        every[b : b + 32, :] = e_ref[HALF * half + 16 : HALF * half + HALF, :]

    near = near_ref[...]
    w_t = w_ref[...]
    far = jnp.maximum(near - ROWS, 0)
    source, within = far >> 4, far & 15
    asks = ask_ref[...].astype(F32).astype(BF16)
    ys[...] = jnp.zeros_like(ys)
    ys[0:K, 0:ROWS] = jnp.where(near >= ROWS, source, me).astype(F32)
    for k in range(K):
        hot = jnp.where(iota((PEERS, ROWS), 0) == source[k : k + 1, :], 1.0, 0.0).astype(BF16)
        picked = dot(asks, hot)
        asked = jnp.sum(jnp.where(iota((16, ROWS), 0) == within[k : k + 1, :], picked, 0.0), axis=0, keepdims=True)
        ys[16 + k : 17 + k, 0:ROWS] = jnp.where(near[k : k + 1, :] >= ROWS, asked, near[k : k + 1, :].astype(F32))
    ys[32 : 32 + K, 0:ROWS] = w_t
    w_hi = w_t.astype(BF16).astype(F32)
    pieces = [ys[0:K, 0:ROWS], ys[16 : 16 + K, 0:ROWS], w_hi, w_t - w_hi]
    xs[...] = jnp.zeros_like(xs)
    for q in range(3):
        for i, piece in enumerate(pieces):
            at = q * 4 * K + i * K
            xs[at : at + K, 0:PACK] = piece[:, q * PACK : (q + 1) * PACK]
    table[...] = xs[...].T[:PACK, :].astype(BF16)
    all_tables[0:PACK, :] = table[...]
    own[...] = ys[...].T

    load_ct.wait()
    column = c * N
    top = jnp.full((ROWS, 1), -1e30, F32)
    for off, width in TILES:
        logits = dot_nt(e_ref[...], ct[off : off + width, :])
        logits = jnp.where(column + off + iota((ROWS, width), 1) < LIVE, logits, -1e30)
        buf1[0:ROWS, off : off + width] = logits
        top = jnp.maximum(top, jnp.max(logits, axis=1, keepdims=True))
    total = jnp.zeros((ROWS, 1), F32)
    for off, width in TILES:
        total += jnp.sum(jnp.exp(buf1[0:ROWS, off : off + width] - top), axis=1, keepdims=True)
    lanes = iota((ROWS, 128), 1)
    xs[...] = jnp.zeros_like(xs)
    xs[0:ROWS, :] = jnp.where(lanes == 0, top, jnp.where(lanes == 1, total, 0.0))
    xt = xs[...].T
    stats[0, :, 0:128] = xt[0:1, :]
    stats[0, :, 128:256] = xt[1:2, :]

    pl.semaphore_wait(barrier, PEERS - 1 + CLS - 1)

    def peer_at(j):
        return {"img": lax.rem(z + 8 - j // 4, 8) * 4 + lax.rem(y + 4 - lax.rem(j, 4), 4)}

    def table_copy(j, n):
        rows = pl.ds(pl.multiple_of(j * PACK, PACK), n * PACK)
        src = table if n == 1 else all_tables.at[rows]
        return pltpu.make_async_remote_copy(src, all_tables.at[rows], table_sem.at[0], table_sem.at[1], device_id=peer_at(j), device_id_type=MESH)

    def send_table(j, carry):
        table_copy(j, 1).start()
        return carry


    y_up, y_down = {"img": z * 4 + lax.rem(y + 1, 4)}, {"img": z * 4 + lax.rem(y + 3, 4)}
    y_far = {"img": z * 4 + lax.rem(y + 2, 4)}
    z_up, z_down = {"img": lax.rem(z + 1, 8) * 4 + y}, {"img": lax.rem(z + 7, 8) * 4 + y}
    sibling = {"cls": c + 1 - 2 * h}
    made = {}

    def go(name, src, dst, n, target, columns=slice(None)):
        i = len(made)
        src = pl.ds(pl.multiple_of(src, 16), n)
        dst = pl.ds(pl.multiple_of(dst, 16), n)
        copy = pltpu.make_async_remote_copy(
            every.at[src, columns], every.at[dst, columns], ssem.at[i], rsem.at[i], device_id=target, device_id_type=MESH
        )
        copy.start()
        made[name] = copy

    def take(*names):
        for name in names:
            made[name].wait_recv()

    def at_a(zi, yi=0):
        return A_AT[zi][0] + A_AT[zi][1] * h + 16 * yi

    def at_b(yi, zi=0):
        return B_AT[yi][zi][0] + B_AT[yi][zi][1] * h

    def share(name, at, n):
        go(name, at, at, n, sibling)

    LEFT, RIGHT = slice(0, 512), slice(512, 1024)

    def a_hop(kind, at, n, old, new):
        go(f"a{kind}{new + 1}", at_a(old + 1) + at, at_a(new + 1) + at, n, z_up)
        go(f"a{kind}{new}", at_a(old) + at, at_a(new) + at, n, z_down)

    def a_first(kind, at, n):
        go(f"a{kind}2", at_a(0) + at, at_a(2) + at, n, z_up)
        go(f"a{kind}1", at_a(0) + at, at_a(1) + at, n, z_down)

    def a_next(kind, at, n, old):
        take(f"a{kind}{old}", f"a{kind}{old + 1}")
        a_hop(kind, at, n, old, old + 2)

    def a_last(kind, at, n):
        take(f"a{kind}5", f"a{kind}6")
        go(f"a{kind}7u", at_a(6) + at, at_a(7) + at, n, z_up, LEFT)
        go(f"a{kind}7d", at_a(5) + at, at_a(7) + at, n, z_down, RIGHT)

    P_ROWS, Q_ROWS = (0, 16), (16, 48)

    def b_next(old):
        take(f"bz{old}", f"bz{old + 1}")
        go(f"bz{old + 3}", at_b(0, old + 1), at_b(0, old + 3), 32, z_up)
        go(f"bz{old + 2}", at_b(0, old), at_b(0, old + 2), 32, z_down)

    def b_side(first, last):
        n = 32 * (last - first)
        go(f"by2{first}", at_b(0, first), at_b(2, first), n, y_up)
        go(f"by1{first}", at_b(0, first), at_b(1, first), n, y_down)

    def b_across(first, last):
        n = 16 * (last - first)
        take(f"by1{first}", f"by2{first}")
        go(f"by3{first}u", at_b(2, first), at_b(3, first), n, y_up)
        go(f"by3{first}d", at_b(1, first) + n, at_b(3, first) + n, n, y_down)

    def events_0():
        go("bz2", at_b(0), at_b(0, 2), 32, z_up)
        go("bz1", at_b(0), at_b(0, 1), 32, z_down)
        go("ay2", at_a(0), at_a(0, 2), 16, y_up)
        go("ay1", at_a(0), at_a(0, 1), 16, y_down)
        a_first("p", *P_ROWS)
        go("ay3", at_a(0), at_a(0, 3), 16, y_far)

    def events_1():
        b_next(1)
        b_side(0, 3)
        a_next("p", *P_ROWS, 1)
        take("ay1", "ay2", "ay3")
        a_first("q", *Q_ROWS)
        share("s0", at_b(0, 1), 64)
        share("r0", at_a(0, 1), 48)

    def events_2():
        b_next(3)
        b_side(3, 5)
        a_next("p", *P_ROWS, 3)
        share("s1", at_b(0, 3), 64)

    def events_3():
        take("bz5", "bz6")
        go("bz7u", at_b(0, 6), at_b(0, 7), 16, z_up)
        go("bz7d", at_b(0, 5) + 16, at_b(0, 7) + 16, 16, z_down)
        b_side(5, 7)
        share("s2", at_b(0, 5), 64)
        a_next("q", *Q_ROWS, 1)
        a_last("p", *P_ROWS)
        b_across(0, 3)
        share("r1", at_a(1), 128)
        share("t10", at_b(1), 96)
        share("t20", at_b(2), 96)

    def events_4():
        take("bz7u", "bz7d")
        b_side(7, 8)
        a_next("q", *Q_ROWS, 3)
        b_across(3, 5)
        share("s3", at_b(0, 7), 32)
        share("r3", at_a(3), 128)
        share("t13", at_b(1, 3), 64)
        share("t23", at_b(2, 3), 64)

    def events_5():
        b_across(5, 7)
        a_last("q", *Q_ROWS)
        share("r5", at_a(5), 128)
        share("t15", at_b(1, 5), 64)
        share("t25", at_b(2, 5), 64)

    def events_6():
        b_across(7, 8)
        take("ap7u", "ap7d", "aq7u", "aq7d")
        share("r7", at_a(7), 64)
        share("t17", at_b(1, 7), 32)
        share("t27", at_b(2, 7), 32)

    def events_7():
        take("by33u", "by33d", "by35u", "by35d")
        share("t33", at_b(3, 3), 128)

    def events_8():
        take("by30u", "by30d", "by37u", "by37d")
        share("t30", at_b(3), 96)
        share("t37", at_b(3, 7), 32)

    lax.fori_loop(1, PEERS, send_table, 0)
    def stat_copy(j, n):
        src = stats.at[0] if n == 1 else stats.at[pl.ds(j, n)]
        dst = stats.at[j] if n == 1 else stats.at[pl.ds(j, n)]
        return pltpu.make_async_remote_copy(
            src, dst, stat_sem.at[0], stat_sem.at[1], device_id={"cls": lax.rem(c + j, CLS)}, device_id_type=MESH
        )

    def send_stat(j, carry):
        stat_copy(j, 1).start()
        return carry

    lax.fori_loop(1, CLS, send_stat, 0)
    events_0()

    stat_copy(1, CLS - 1).wait_recv()
    top = stats[0, :, 0:128]
    for j in range(1, CLS):
        top = jnp.maximum(top, stats[j, :, 0:128])
    total = jnp.zeros((1, 128), F32)
    for j in range(CLS):
        total += stats[j, :, 128:256] * jnp.exp(stats[j, :, 0:128] - top)
    lses[0] = top + jnp.log(total)

    def lse_copy(j, n):
        src = lses.at[0] if n == 1 else lses.at[pl.ds(j, n)]
        dst = lses.at[j] if n == 1 else lses.at[pl.ds(j, n)]
        return pltpu.make_async_remote_copy(src, dst, lse_sem.at[0], lse_sem.at[1], device_id=peer_at(j), device_id_type=MESH)

    def send_lse(j, carry):
        lse_copy(j, 1).start()
        return carry

    lax.fori_loop(1, PEERS, send_lse, 0)

    events_1()


    table_copy(1, PEERS - 1).wait_recv()
    mine = own[pl.ds(pl.multiple_of(HALF * h, 16), HALF), :]
    lanes = iota((HALF, 128), 1)
    peer = mine.astype(jnp.int32)
    row = pltpu.roll(mine, 128 - 16, 1).astype(jnp.int32)
    weight = pltpu.roll(mine, 128 - 32, 1)
    scale = 1.0 / (1.0 + jnp.sum(jnp.where(lanes < K, weight, 0.0), axis=1, keepdims=True))
    dz, dy = relative(z, y, peer)
    packed = (dz * 4 + dy) * PACK + (row & (PACK - 1))
    group = row >> 5
    for step in range(4):
        at = iota((HALF, 256), 1) + step * 256
        hot = [jnp.where(at == packed[:, k : k + 1], 1.0, 0.0).astype(BF16) for k in range(K)]
        part = dot(jnp.concatenate(hot, axis=0), all_tables[step * 256 : step * 256 + 256, :])
        got[...] = part if step == 0 else got[...] + part
    peers = jnp.zeros((HALF, 128), F32)
    rows = jnp.zeros((HALF, 128), F32)
    values = jnp.zeros((HALF, 128), F32)
    for k in range(K):
        g = got[k * HALF : (k + 1) * HALF, :]
        q = group[:, k : k + 1]
        g = jnp.where(q == 0, g, jnp.where(q == 1, pltpu.roll(g, 128 - 4 * K, 1), pltpu.roll(g, 128 - 8 * K, 1)))
        edge = jnp.where(lanes < K, pltpu.roll(g, 128 - 2 * K, 1) + pltpu.roll(g, 128 - 3 * K, 1), 0.0)
        outer = weight[:, k : k + 1] / (1.0 + jnp.sum(edge, axis=1, keepdims=True))
        self_lane = lanes == K
        pk = jnp.where(self_lane, peer[:, k : k + 1].astype(F32), jnp.where(lanes < K, g, 0.0))
        rk = jnp.where(self_lane, row[:, k : k + 1].astype(F32), jnp.where(lanes < K, pltpu.roll(g, 128 - K, 1), 0.0))
        vk = jnp.where(self_lane, outer, edge * outer)
        if k:
            pk, rk, vk = pltpu.roll(pk, 12 * k, 1), pltpu.roll(rk, 12 * k, 1), pltpu.roll(vk, 12 * k, 1)
        peers, rows, values = peers + pk, rows + rk, values + vk
    itself = lanes == 12 * K
    peers = jnp.where(itself, me, peers.astype(jnp.int32))
    rows = jnp.where(itself, HALF * h + iota((HALF, 128), 0), rows.astype(jnp.int32))
    where = place(z, y, peers, rows)
    lists_a[...] = where >> 7
    lists_b[...] = where & 127
    lists_v[...] = jnp.where(itself, 1.0, values) * scale
    events_2()

    def scatter(r, carry):
        a, b, v = lists_a[pl.ds(r, 1), :], lists_b[pl.ds(r, 1), :], lists_v[pl.ds(r, 1), :]
        left = jnp.where(iota((32, 128), 0) == a, v, 0.0)
        right = jnp.where(iota((128, 128), 0) == b, 1.0, 0.0).astype(BF16)
        out = dot_nt(jnp.concatenate(split(left), axis=0), right)
        dense[pl.ds(r, 24, stride=HALF), :] = out[:24] + out[32:56]
        return carry

    lax.fori_loop(0, HALF // 2, scatter, 0, unroll=8)
    events_3()
    lax.fori_loop(HALF // 2, HALF, scatter, 0, unroll=8)
    mine_hi = pl.ds(pl.multiple_of(HALF * h, 16), HALF)
    mine_lo = pl.ds(pl.multiple_of(HALF * h + ROWS, 16), HALF)
    for i in range(ALL // 128):
        hi, lo = split(dense[i * HALF : (i + 1) * HALF, :])
        m_ref[mine_hi, i * 128 : (i + 1) * 128] = hi
        m_ref[mine_lo, i * 128 : (i + 1) * 128] = lo
    m_copies = [
        pltpu.make_async_remote_copy(
            m_ref.at[part], m_ref.at[part], m_sem.at[i, 0], m_sem.at[i, 1], device_id=sibling, device_id_type=MESH
        )
        for i, part in enumerate((mine_hi, mine_lo))
    ]
    for copy in m_copies:
        copy.start()

    lse_copy(1, PEERS - 1).wait_recv()
    xs[...] = jnp.zeros_like(xs)
    xs[0:PEERS, :] = lses[:, 0, :]
    ys[...] = xs[...].T
    for dz in range(8):
        for dy in range(4):
            zi = 0 if dz == 0 else 2 * dz - 1 if dz <= 4 else 16 - 2 * dz
            yi = dy if dy < 2 else 5 - dy
            for half in range(2):
                col = jnp.broadcast_to(ys[HALF * half : HALF * half + HALF, dz * 4 + dy : dz * 4 + dy + 1], (HALF, 128))
                a = A_AT[zi][0] + A_AT[zi][1] * half + 16 * yi
                b = B_AT[yi][zi][0] + B_AT[yi][zi][1] * half
                lse_ref[a : a + 16, :] = col[:16]
                lse_ref[b : b + 32, :] = col[16:]
    acc[...] = jnp.zeros_like(acc)
    def logits_tile(chunk, off, width):
        first, last = CHUNK_AT[chunk], CHUNK_AT[chunk + 1]
        bufs[chunk % 2][: last - first, off : off + width] = dot_nt(every[first:last, :], ct[off : off + width, :])

    def label_tile(chunk, off, width):
        first, last = CHUNK_AT[chunk], CHUNK_AT[chunk + 1]
        lse = lse_ref[first:last, :]
        lse = jnp.concatenate([lse] * (-(-width // 128)), axis=1)[:, :width]
        hi, lo = split(jnp.exp(bufs[chunk % 2][: last - first, off : off + width] - lse))
        m = m_ref[:, first:last]
        a = dot(m, hi)
        acc[:, off : off + width] += a[:ROWS] + a[ROWS:] + dot(m[:ROWS], lo)

    def wait_matrix():
        for copy in m_copies:
            copy.wait_recv()

    arrivals = [
        ("r0", "s0", "s1", "s2"),
        ("r1", "t10", "t20"),
        ("s3", "r3", "t13", "t23"),
        ("r5", "t15", "t25"),
        ("r7", "t17", "t27", "t33"),
        ("t30", "t37"),
    ]
    events = {
        (-1, 5): events_4,
        (0, 0): wait_matrix,
        (0, 5): events_5,
        (1, 4): events_6,
        (2, 0): events_7,
        (2, 8): events_8,
    }
    for chunk in range(-1, CHUNKS):
        if chunk + 1 < CHUNKS:
            take(*arrivals[chunk + 1])
        for i, (off, width) in enumerate(TILES):
            if (chunk, i) in events:
                events[chunk, i]()
            if chunk + 1 < CHUNKS:
                logits_tile(chunk + 1, off, width)
            if chunk >= 0:
                label_tile(chunk, off, width)
    for off, width in TILES:
        here = column + off + iota((ROWS, width), 1)
        o_ref[:, off : off + width] = jnp.where(here < LIVE, acc[:, off : off + width], 0.0)

    for copy in made.values():
        copy.wait_send()
    for copy in m_copies:
        copy.wait_send()
    table_copy(1, PEERS - 1).wait_send()
    stat_copy(1, CLS - 1).wait_send()
    lse_copy(1, PEERS - 1).wait_send()


def shards(embeddings, class_text_embedding, neighbours, weights, requests):
    vmem = pl.BlockSpec(memory_space=pltpu.VMEM)
    dma = pltpu.SemaphoreType.DMA
    return pl.pallas_call(
        kernel,
        out_shape=jax.ShapeDtypeStruct((ROWS, N), F32),
        in_specs=[vmem, pl.BlockSpec(memory_space=pl.ANY), vmem, vmem, vmem],
        out_specs=vmem,
        scratch_shapes=[
            pltpu.VMEM((ALL, D), BF16),
            pltpu.VMEM((N, D), BF16),
            pltpu.VMEM((CHUNK, N), F32),
            pltpu.VMEM((CHUNK, N), F32),
            pltpu.VMEM((ROWS, N), F32),
            pltpu.VMEM((ALL, 128), F32),
            pltpu.VMEM((2 * ROWS, ALL), BF16),
            pltpu.VMEM((24 * HALF, 128), F32),
            pltpu.VMEM((PACK, 128), BF16),
            pltpu.VMEM((PEERS * PACK, 128), BF16),
            pltpu.VMEM((128, 128), F32),
            pltpu.VMEM((128, 128), F32),
            pltpu.VMEM((128, 128), F32),
            pltpu.VMEM((HALF, 128), jnp.int32),
            pltpu.VMEM((HALF, 128), jnp.int32),
            pltpu.VMEM((HALF, 128), F32),
            pltpu.VMEM((K * HALF, 128), F32),
            pltpu.VMEM((CLS, 1, 256), F32),
            pltpu.VMEM((PEERS, 1, 128), F32),
            dma,
            dma((MESSAGES,)),
            dma((MESSAGES,)),
            dma((2,)),
            dma((2,)),
            dma((2,)),
            dma((2, 2)),
        ],
        compiler_params=pltpu.CompilerParams(vmem_limit_bytes=56 << 20, collective_id=0, has_side_effects=True),
    )(embeddings, class_text_embedding.T, neighbours.T, weights.T, requests[0].T)


def solution(mesh):
    in_specs = (
        P("img", None),
        P(None, "cls"),
        P("img", None),
        P("img", None),
        P("img", None, None),
    )
    return jax.shard_map(shards, mesh=mesh, in_specs=in_specs, out_specs=P("img", "cls"), check_vma=False)
```

```python
import jax
import jax.numpy as jnp
from jax import lax
from jax.experimental import pallas as pl
from jax.experimental.pallas import tpu as pltpu
from jax.sharding import PartitionSpec as P

LIVE = 21841
ROWS = 96
HALF = 48
K = 10
PEERS = 32
CLS = 8
ALL = ROWS * PEERS
D = 1024
N = 2736
TN = 256
PACK = 32
F32 = jnp.float32
BF16 = jnp.bfloat16
MESH = pl.DeviceIdType.MESH
TILES = [(off, min(TN, N - off)) for off in range(0, N, TN)]
A_AT = [(0, 64)] + [(s + 64 * i, 128) for s in (384, 1280, 1664) for i in range(2)] + [(2304, 64)]
B_AT = [
    [(128 + 32 * i, 128) for i in range(4)] + [(1024 + 32 * i, 128) for i in range(4)],
    [(640 + 32 * i, 96) for i in range(3)] + [(1536, 32)] + [(1920 + 32 * i, 96) for i in range(3)] + [(2432, 32)],
    [(832 + 32 * i, 96) for i in range(3)] + [(1600, 32)] + [(2112 + 32 * i, 96) for i in range(3)] + [(2496, 32)],
    [(2560 + 32 * i, 96) for i in range(3)] + [(2752, 32)] + [(2816 + 32 * i, 96) for i in range(3)] + [(3008, 32)],
]
CHUNK_AT = (0, 384, 1024, 1664, 2304, 2816, 3072)
CHUNKS = 6
CHUNK = 640
MESSAGES = 72


def dot(a, b):
    return jnp.dot(a, b, preferred_element_type=F32)


def dot_nt(a, b):
    return lax.dot_general(a, b, (((1,), (1,)), ((), ())), preferred_element_type=F32)


def split(x):
    hi = x.astype(BF16)
    return hi, (x - hi.astype(F32)).astype(BF16)


def iota(shape, axis):
    return lax.broadcasted_iota(jnp.int32, shape, axis)


def relative(z, y, peer):
    return ((peer >> 2) - z) & 7, ((peer & 3) - y) & 3


def place(z, y, peer, row):
    dz, dy = relative(z, y, peer)
    zi = jnp.where(dz == 0, 0, jnp.where(dz <= 4, 2 * dz - 1, 16 - 2 * dz))
    yi = jnp.where(dy < 2, dy, 5 - dy)
    half = jnp.where(row >= HALF, 1, 0)
    t = row - HALF * half
    a, b = jnp.zeros_like(t), jnp.zeros_like(t)
    for i in range(8):
        a = jnp.where(zi == i, A_AT[i][0] + A_AT[i][1] * half, a)
        for j in range(4):
            b = jnp.where(jnp.logical_and(zi == i, yi == j), B_AT[j][i][0] + B_AT[j][i][1] * half, b)
    return jnp.where(t < 16, a + 16 * yi + t, b + t - 16)


def kernel(
    e_ref, ct_hbm, near_ref, w_ref, ask_ref, o_ref,
    every, ct, buf0, buf1, lse_ref, m_ref, dense, table, all_tables, own, xs, ys, lists_a, lists_b, lists_v, hots, got, stats, lses,
    ct_sem, ssem, rsem, table_sem, stat_sem, lse_sem, m_sem,
):
    me, c = lax.axis_index("img"), lax.axis_index("cls")
    z, y, h = me // 4, lax.rem(me, 4), lax.rem(c, 2)
    bufs = (buf0, buf1)

    load_ct = pltpu.make_async_copy(ct_hbm, ct, ct_sem)
    load_ct.start()

    barrier = pltpu.get_barrier_semaphore()

    def greet_img(j, carry):
        pl.semaphore_signal(barrier, inc=1, device_id={"img": lax.rem(me + j, PEERS)}, device_id_type=MESH)
        return carry

    def greet_cls(j, carry):
        pl.semaphore_signal(barrier, inc=1, device_id={"cls": lax.rem(c + j, CLS)}, device_id_type=MESH)
        return carry

    lax.fori_loop(1, PEERS, greet_img, 0)
    lax.fori_loop(1, CLS, greet_cls, 0)

    for half in range(2):
        a, b = A_AT[0][0] + A_AT[0][1] * half, B_AT[0][0][0] + B_AT[0][0][1] * half
        every[a : a + 16, :] = e_ref[HALF * half : HALF * half + 16, :]
        every[b : b + 32, :] = e_ref[HALF * half + 16 : HALF * half + HALF, :]

    near = near_ref[...]
    w_t = w_ref[...]
    far = jnp.maximum(near - ROWS, 0)
    source, within = far >> 4, far & 15
    asks = ask_ref[...].astype(F32).astype(BF16)
    ys[...] = jnp.zeros_like(ys)
    ys[0:K, 0:ROWS] = jnp.where(near >= ROWS, source, me).astype(F32)
    for k in range(K):
        hot = jnp.where(iota((PEERS, ROWS), 0) == source[k : k + 1, :], 1.0, 0.0).astype(BF16)
        picked = dot(asks, hot)
        asked = jnp.sum(jnp.where(iota((16, ROWS), 0) == within[k : k + 1, :], picked, 0.0), axis=0, keepdims=True)
        ys[16 + k : 17 + k, 0:ROWS] = jnp.where(near[k : k + 1, :] >= ROWS, asked, near[k : k + 1, :].astype(F32))
    ys[32 : 32 + K, 0:ROWS] = w_t
    w_hi = w_t.astype(BF16).astype(F32)
    pieces = [ys[0:K, 0:ROWS], ys[16 : 16 + K, 0:ROWS], w_hi, w_t - w_hi]
    xs[...] = jnp.zeros_like(xs)
    for q in range(3):
        for i, piece in enumerate(pieces):
            at = q * 4 * K + i * K
            xs[at : at + K, 0:PACK] = piece[:, q * PACK : (q + 1) * PACK]
    table[...] = xs[...].T[:PACK, :].astype(BF16)
    all_tables[0] = table[...]
    own[...] = ys[...].T

    load_ct.wait()
    column = c * N
    top = jnp.full((ROWS, 1), -1e30, F32)
    for off, width in TILES:
        logits = dot_nt(e_ref[...], ct[off : off + width, :])
        logits = jnp.where(column + off + iota((ROWS, width), 1) < LIVE, logits, -1e30)
        buf1[0:ROWS, off : off + width] = logits
        top = jnp.maximum(top, jnp.max(logits, axis=1, keepdims=True))
    total = jnp.zeros((ROWS, 1), F32)
    for off, width in TILES:
        total += jnp.sum(jnp.exp(buf1[0:ROWS, off : off + width] - top), axis=1, keepdims=True)
    lanes = iota((ROWS, 128), 1)
    xs[...] = jnp.zeros_like(xs)
    xs[0:ROWS, :] = jnp.where(lanes == 0, top, jnp.where(lanes == 1, total, 0.0))
    xt = xs[...].T
    stats[0, :, 0:128] = xt[0:1, :]
    stats[0, :, 128:256] = xt[1:2, :]


    mine = own[pl.ds(pl.multiple_of(HALF * h, 16), HALF), :]
    lanes = iota((HALF, 128), 1)
    peer = mine.astype(jnp.int32)
    row = pltpu.roll(mine, 128 - 16, 1).astype(jnp.int32)
    weight = pltpu.roll(mine, 128 - 32, 1)
    scale = 1.0 / (1.0 + jnp.sum(jnp.where(lanes < K, weight, 0.0), axis=1, keepdims=True))
    dz, dy = relative(z, y, peer)
    packed = (dz * 4 + dy) * PACK + (row & (PACK - 1))
    group = row >> 5
    for k in range(K):
        at = iota((HALF, PEERS * PACK), 1)
        hots[k * HALF : (k + 1) * HALF, :] = jnp.where(at == packed[:, k : k + 1], 1.0, 0.0).astype(BF16)

    pl.semaphore_wait(barrier, PEERS - 1 + CLS - 1)

    def peer_at(j):
        return {"img": lax.rem(z + 8 - j // 4, 8) * 4 + lax.rem(y + 4 - lax.rem(j, 4), 4)}

    table_half = pl.ds(pl.multiple_of(h * (PACK // 2), 16), PACK // 2)

    def table_copy(j, n):
        src = table.at[table_half] if n == 1 else all_tables.at[pl.ds(j, n), table_half]
        dst = all_tables.at[j, table_half] if n == 1 else all_tables.at[pl.ds(j, n), table_half]
        return pltpu.make_async_remote_copy(src, dst, table_sem.at[0], table_sem.at[1], device_id=peer_at(j), device_id_type=MESH)

    def send_table(j, carry):
        table_copy(j, 1).start()
        return carry


    y_up, y_down = {"img": z * 4 + lax.rem(y + 1, 4)}, {"img": z * 4 + lax.rem(y + 3, 4)}
    y_far = {"img": z * 4 + lax.rem(y + 2, 4)}
    z_up, z_down = {"img": lax.rem(z + 1, 8) * 4 + y}, {"img": lax.rem(z + 7, 8) * 4 + y}
    sibling = {"cls": c + 1 - 2 * h}
    made = {}

    def go(name, src, dst, n, target, columns=slice(None)):
        i = len(made)
        src = pl.ds(pl.multiple_of(src, 16), n)
        dst = pl.ds(pl.multiple_of(dst, 16), n)
        copy = pltpu.make_async_remote_copy(
            every.at[src, columns], every.at[dst, columns], ssem.at[i], rsem.at[i], device_id=target, device_id_type=MESH
        )
        copy.start()
        made[name] = copy

    def take(*names):
        for name in names:
            made[name].wait_recv()

    def at_a(zi, yi=0):
        return A_AT[zi][0] + A_AT[zi][1] * h + 16 * yi

    def at_b(yi, zi=0):
        return B_AT[yi][zi][0] + B_AT[yi][zi][1] * h

    def share(name, at, n):
        go(name, at, at, n, sibling)

    LEFT, RIGHT = slice(0, 512), slice(512, 1024)

    def a_hop(kind, at, n, old, new):
        go(f"a{kind}{new + 1}", at_a(old + 1) + at, at_a(new + 1) + at, n, z_up)
        go(f"a{kind}{new}", at_a(old) + at, at_a(new) + at, n, z_down)

    def a_first(kind, at, n):
        go(f"a{kind}2", at_a(0) + at, at_a(2) + at, n, z_up)
        go(f"a{kind}1", at_a(0) + at, at_a(1) + at, n, z_down)

    def a_next(kind, at, n, old):
        take(f"a{kind}{old}", f"a{kind}{old + 1}")
        a_hop(kind, at, n, old, old + 2)

    def a_last(kind, at, n):
        take(f"a{kind}5", f"a{kind}6")
        go(f"a{kind}7u", at_a(6) + at, at_a(7) + at, n, z_up, LEFT)
        go(f"a{kind}7d", at_a(5) + at, at_a(7) + at, n, z_down, RIGHT)

    P_ROWS, Q_ROWS = (0, 16), (16, 48)

    def b_next(old):
        take(f"bz{old}", f"bz{old + 1}")
        go(f"bz{old + 3}", at_b(0, old + 1), at_b(0, old + 3), 32, z_up)
        go(f"bz{old + 2}", at_b(0, old), at_b(0, old + 2), 32, z_down)

    def b_side(first, last):
        n = 32 * (last - first)
        go(f"by2{first}", at_b(0, first), at_b(2, first), n, y_up)
        go(f"by1{first}", at_b(0, first), at_b(1, first), n, y_down)

    def b_across(first, last):
        n = 16 * (last - first)
        take(f"by1{first}", f"by2{first}")
        go(f"by3{first}u", at_b(2, first), at_b(3, first), n, y_up)
        go(f"by3{first}d", at_b(1, first) + n, at_b(3, first) + n, n, y_down)

    def events_0():
        go("bz2", at_b(0), at_b(0, 2), 32, z_up)
        go("bz1", at_b(0), at_b(0, 1), 32, z_down)
        go("ay2", at_a(0), at_a(0, 2), 16, y_up)
        go("ay1", at_a(0), at_a(0, 1), 16, y_down)
        a_first("p", *P_ROWS)
        go("ay3", at_a(0), at_a(0, 3), 16, y_far)

    def events_1():
        b_next(1)
        b_side(0, 3)
        a_next("p", *P_ROWS, 1)
        take("ay1", "ay2", "ay3")
        a_first("q", *Q_ROWS)
        share("s0", at_b(0, 1), 64)
        share("r0", at_a(0, 1), 48)

    def events_2():
        b_next(3)
        b_side(3, 4)
        share("s1", at_b(0, 3), 32)
        a_next("p", *P_ROWS, 3)

    def events_3():
        take("bz5", "bz6")
        go("bz7u", at_b(0, 6), at_b(0, 7), 16, z_up)
        go("bz7d", at_b(0, 5) + 16, at_b(0, 7) + 16, 16, z_down)
        b_side(4, 7)
        a_next("q", *Q_ROWS, 1)
        a_last("p", *P_ROWS)
        b_across(0, 3)
        share("r1", at_a(1), 128)
        share("t10", at_b(1), 96)
        share("t20", at_b(2), 96)
        share("s2", at_b(0, 4), 96)

    def events_4():
        take("bz7u", "bz7d")
        b_side(7, 8)
        a_next("q", *Q_ROWS, 3)
        b_across(3, 4)
        share("r3", at_a(3), 128)
        share("t13", at_b(1, 3), 32)
        share("t23", at_b(2, 3), 32)
        share("s3", at_b(0, 7), 32)

    def events_5():
        b_across(4, 7)
        a_last("q", *Q_ROWS)
        share("r5", at_a(5), 128)
        share("t14", at_b(1, 4), 96)
        share("t24", at_b(2, 4), 96)

    def events_6():
        b_across(7, 8)
        take("ap7u", "ap7d", "aq7u", "aq7d")
        share("r7", at_a(7), 64)
        share("t17", at_b(1, 7), 32)
        share("t27", at_b(2, 7), 32)

    def events_7():
        take("by30u", "by30d", "by33u", "by33d")
        share("t30", at_b(3), 96)
        share("t33", at_b(3, 3), 32)

    def events_8():
        take("by34u", "by34d", "by37u", "by37d")
        share("t34", at_b(3, 4), 96)
        share("t37", at_b(3, 7), 32)

    lax.fori_loop(1, PEERS, send_table, 0)
    def stat_copy(j, n):
        src = stats.at[0] if n == 1 else stats.at[pl.ds(j, n)]
        dst = stats.at[j] if n == 1 else stats.at[pl.ds(j, n)]
        return pltpu.make_async_remote_copy(
            src, dst, stat_sem.at[0], stat_sem.at[1], device_id={"cls": lax.rem(c + j, CLS)}, device_id_type=MESH
        )

    def send_stat(j, carry):
        stat_copy(j, 1).start()
        return carry

    lax.fori_loop(1, CLS, send_stat, 0)
    events_0()

    stat_copy(1, CLS - 1).wait_recv()
    top = stats[0, :, 0:128]
    for j in range(1, CLS):
        top = jnp.maximum(top, stats[j, :, 0:128])
    total = jnp.zeros((1, 128), F32)
    for j in range(CLS):
        total += stats[j, :, 128:256] * jnp.exp(stats[j, :, 0:128] - top)
    lses[0] = top + jnp.log(total)

    def lse_copy(j, n):
        src = lses.at[0] if n == 1 else lses.at[pl.ds(j, n)]
        dst = lses.at[j] if n == 1 else lses.at[pl.ds(j, n)]
        return pltpu.make_async_remote_copy(src, dst, lse_sem.at[0], lse_sem.at[1], device_id=peer_at(j), device_id_type=MESH)

    def send_lse(j, carry):
        lse_copy(j, 1).start()
        return carry

    lax.fori_loop(1, PEERS, send_lse, 0)


    table_copy(1, PEERS - 1).wait_recv()
    others = all_tables.at[pl.ds(1, PEERS - 1), table_half]
    table_share = pltpu.make_async_remote_copy(others, others, table_sem.at[2], table_sem.at[3], device_id=sibling, device_id_type=MESH)
    table_share.start()
    events_1()
    table_share.wait_recv()
    got[...] = dot(hots[...], jnp.concatenate([all_tables[j] for j in range(PEERS)], axis=0))
    peers = jnp.zeros((HALF, 128), F32)
    rows = jnp.zeros((HALF, 128), F32)
    values = jnp.zeros((HALF, 128), F32)
    for k in range(K):
        g = got[k * HALF : (k + 1) * HALF, :]
        q = group[:, k : k + 1]
        g = jnp.where(q == 0, g, jnp.where(q == 1, pltpu.roll(g, 128 - 4 * K, 1), pltpu.roll(g, 128 - 8 * K, 1)))
        edge = jnp.where(lanes < K, pltpu.roll(g, 128 - 2 * K, 1) + pltpu.roll(g, 128 - 3 * K, 1), 0.0)
        outer = weight[:, k : k + 1] / (1.0 + jnp.sum(edge, axis=1, keepdims=True))
        self_lane = lanes == K
        pk = jnp.where(self_lane, peer[:, k : k + 1].astype(F32), jnp.where(lanes < K, g, 0.0))
        rk = jnp.where(self_lane, row[:, k : k + 1].astype(F32), jnp.where(lanes < K, pltpu.roll(g, 128 - K, 1), 0.0))
        vk = jnp.where(self_lane, outer, edge * outer)
        if k:
            pk, rk, vk = pltpu.roll(pk, 12 * k, 1), pltpu.roll(rk, 12 * k, 1), pltpu.roll(vk, 12 * k, 1)
        peers, rows, values = peers + pk, rows + rk, values + vk
    itself = lanes == 12 * K
    peers = jnp.where(itself, me, peers.astype(jnp.int32))
    rows = jnp.where(itself, HALF * h + iota((HALF, 128), 0), rows.astype(jnp.int32))
    where = place(z, y, peers, rows)
    lists_a[...] = where >> 7
    lists_b[...] = where & 127
    lists_v[...] = jnp.where(itself, 1.0, values) * scale
    events_2()

    def scatter(r, carry):
        a, b, v = lists_a[pl.ds(r, 1), :], lists_b[pl.ds(r, 1), :], lists_v[pl.ds(r, 1), :]
        left = jnp.where(iota((32, 128), 0) == a, v, 0.0)
        right = jnp.where(iota((128, 128), 0) == b, 1.0, 0.0).astype(BF16)
        out = dot_nt(jnp.concatenate(split(left), axis=0), right)
        dense[pl.ds(r, 24, stride=HALF), :] = out[:24] + out[32:56]
        return carry

    lax.fori_loop(0, HALF, scatter, 0, unroll=24)
    mine_hi = pl.ds(pl.multiple_of(HALF * h, 16), HALF)
    mine_lo = pl.ds(pl.multiple_of(HALF * h + ROWS, 16), HALF)
    for i in range(ALL // 128):
        hi, lo = split(dense[i * HALF : (i + 1) * HALF, :])
        m_ref[mine_hi, i * 128 : (i + 1) * 128] = hi
        m_ref[mine_lo, i * 128 : (i + 1) * 128] = lo
    m_copies = [
        pltpu.make_async_remote_copy(
            m_ref.at[part], m_ref.at[part], m_sem.at[i, 0], m_sem.at[i, 1], device_id=sibling, device_id_type=MESH
        )
        for i, part in enumerate((mine_hi, mine_lo))
    ]
    for copy in m_copies:
        copy.start()

    lse_copy(1, PEERS - 1).wait_recv()
    xs[...] = jnp.zeros_like(xs)
    xs[0:PEERS, :] = lses[:, 0, :]
    ys[...] = xs[...].T

    def expand(j):
        dz, dy = j // 4, j % 4
        zi = 0 if dz == 0 else 2 * dz - 1 if dz <= 4 else 16 - 2 * dz
        yi = dy if dy < 2 else 5 - dy
        for half in range(2):
            col = jnp.broadcast_to(ys[HALF * half : HALF * half + HALF, j : j + 1], (HALF, 128))
            a = A_AT[zi][0] + A_AT[zi][1] * half + 16 * yi
            b = B_AT[yi][zi][0] + B_AT[yi][zi][1] * half
            lse_ref[a : a + 16, :] = col[:16]
            lse_ref[b : b + 32, :] = col[16:]

    o_ref[...] = jnp.zeros_like(o_ref)
    def logits_tile(chunk, off, width):
        first, last = CHUNK_AT[chunk], CHUNK_AT[chunk + 1]
        bufs[chunk % 2][: last - first, off : off + width] = dot_nt(every[first:last, :], ct[off : off + width, :])

    def label_tile(chunk, off, width):
        first, last = CHUNK_AT[chunk], CHUNK_AT[chunk + 1]
        lse = lse_ref[first:last, :]
        lse = jnp.concatenate([lse] * (-(-width // 128)), axis=1)[:, :width]
        hi, lo = split(jnp.exp(bufs[chunk % 2][: last - first, off : off + width] - lse))
        m = m_ref[:, first:last]
        a = dot(m, hi)
        o_ref[:, off : off + width] += a[:ROWS] + a[ROWS:] + dot(m[:ROWS], lo)

    def wait_matrix():
        for copy in m_copies:
            copy.wait_recv()

    arrivals = [
        ("r0", "s0", "s1"),
        ("r1", "t10", "t20"),
        ("s2", "s3", "r3", "t13", "t23"),
        ("r5", "t14", "t24"),
        ("r7", "t17", "t27", "t30", "t33"),
        ("t34", "t37"),
    ]
    events = {
        (-1, 6): events_3,
        (0, 0): wait_matrix,
        (0, 6): events_4,
        (1, 5): events_5,
        (2, 2): events_6,
        (2, 6): events_7,
        (3, 2): events_8,
    }
    for chunk in range(-1, CHUNKS):
        if chunk + 1 < CHUNKS:
            take(*arrivals[chunk + 1])
        for i, (off, width) in enumerate(TILES):
            if (chunk, i) in events:
                events[chunk, i]()
            if chunk + 1 < CHUNKS:
                logits_tile(chunk + 1, off, width)
            if chunk >= 0:
                label_tile(chunk, off, width)
            else:
                for j in range(3 * i, min(3 * i + 3, PEERS)):
                    expand(j)
    for copy in made.values():
        copy.wait_send()
    for copy in m_copies:
        copy.wait_send()
    table_copy(1, PEERS - 1).wait_send()
    table_share.wait_send()
    stat_copy(1, CLS - 1).wait_send()
    lse_copy(1, PEERS - 1).wait_send()


def shards(embeddings, class_text_embedding, neighbours, weights, requests):
    vmem = pl.BlockSpec(memory_space=pltpu.VMEM)
    dma = pltpu.SemaphoreType.DMA
    live = lax.axis_index("cls") * N + jnp.arange(N) < LIVE
    labels = pl.pallas_call(
        kernel,
        out_shape=jax.ShapeDtypeStruct((ROWS, N), F32),
        in_specs=[vmem, pl.BlockSpec(memory_space=pl.ANY), vmem, vmem, vmem],
        out_specs=vmem,
        scratch_shapes=[
            pltpu.VMEM((ALL, D), BF16),
            pltpu.VMEM((N, D), BF16),
            pltpu.VMEM((CHUNK, N), F32),
            pltpu.VMEM((CHUNK, N), F32),
            pltpu.VMEM((ALL, 128), F32),
            pltpu.VMEM((2 * ROWS, ALL), BF16),
            pltpu.VMEM((24 * HALF, 128), F32),
            pltpu.VMEM((PACK, 128), BF16),
            pltpu.VMEM((PEERS, PACK, 128), BF16),
            pltpu.VMEM((128, 128), F32),
            pltpu.VMEM((128, 128), F32),
            pltpu.VMEM((128, 128), F32),
            pltpu.VMEM((HALF, 128), jnp.int32),
            pltpu.VMEM((HALF, 128), jnp.int32),
            pltpu.VMEM((HALF, 128), F32),
            pltpu.VMEM((K * HALF, PEERS * PACK), BF16),
            pltpu.VMEM((K * HALF, 128), F32),
            pltpu.VMEM((CLS, 1, 256), F32),
            pltpu.VMEM((PEERS, 1, 128), F32),
            dma,
            dma((MESSAGES,)),
            dma((MESSAGES,)),
            dma((4,)),
            dma((2,)),
            dma((2,)),
            dma((2, 2)),
        ],
        compiler_params=pltpu.CompilerParams(vmem_limit_bytes=56 << 20, collective_id=0, has_side_effects=True),
    )(embeddings, class_text_embedding.T, neighbours.T, weights.T, requests[0].T)
    return jnp.where(live[None, :], labels, 0.0)


def solution(mesh):
    in_specs = (
        P("img", None),
        P(None, "cls"),
        P("img", None),
        P("img", None),
        P("img", None, None),
    )
    return jax.shard_map(shards, mesh=mesh, in_specs=in_specs, out_specs=P("img", "cls"), check_vma=False)
```
